256 devices in a mesh: grp: 4 (over z_lo), dp: 8 (over y, z_hi), width: 8 (over x, core).
Axes of the slice: x: 4, y: 4, z: 8 (z_hi: 2, z_lo: 4; z = z_hi * 4 + z_lo), core: 2. Of those that a mesh axis runs over, the one named last changes fastest.
Arguments:
- query_out: bfloat16 [512, 8192], P(None, ('grp', 'dp')), may hold values from -0.125 to 0.125
- query_in: bfloat16 [512, 14336], P(None, 'width'), may hold values from -0.046875 to 0.046875
- eigen_out: bfloat16 [8192, 8192], P(('grp', 'dp'), 'width'), may hold values from -0.0625 to 0.0625
- eigen_in: bfloat16 [14336, 14336], P('width', ('grp', 'dp')), may hold values from -0.046875 to 0.046875
- eigvals: float32 [8192, 14336], P('width', ('grp', 'dp')), may hold values from 0.001 to 5
- start: bfloat16 [14336, 256], P(('grp', 'dp')), may hold values from -6 to 6
- grads_out: bfloat16 [16384, 8192], P(('grp', 'dp'), 'width'), may hold values from -0.0625 to 0.0625
- gate_pre: bfloat16 [16384, 14336], P(('grp', 'dp'), 'width'), may hold values from -6 to 6
- up_pre: bfloat16 [16384, 14336], P(('grp', 'dp'), 'width'), may hold values from -0.046875 to 0.046875
Outputs:
- scores: float32 [16, 16384], P(None, ('grp', 'dp', 'width'))
- out_factor: bfloat16 [8192, 256], P('width')
- in_factor: bfloat16 [14336, 256], P('width')
The draws below stay inside these ranges and needn't reach their ends.
All inputs are finite; a program needn't handle non-finite values.
Results may differ from the reference program's by a relative error of at most 0.0095.
Values may be sent and summed in bfloat16 or wider, within the bound.
A program may use at most 128 MiB of HBM per device.

```python
import jax
import jax.numpy as jnp
from jax import lax

D = 8192
FF = 14336
NQ = 16
QTOK = 32
RANK = 16
ITERS = 2
KQ = 512
TOKENS = 16384
N_GRP = 4
N_DP = 8


def draw_eigvals(key, part):
    block_count = N_GRP * N_DP
    width_block = FF // block_count
    chosen_block = jax.random.randint(jax.random.fold_in(key, 7), (), 0, block_count)
    uniform_draw = jax.random.uniform(jax.random.fold_in(key, 11), (D, FF), jnp.float32)
    base_values = 0.05 * 100.0 ** uniform_draw
    column_block = jnp.arange(FF) // width_block
    scale_factor = jnp.where(column_block == chosen_block, 0.02, 1.0).astype(jnp.float32)
    return base_values * scale_factor[None, :]


def spiked(entries, key, source, target, shards_of, factor):
    owner, partner = [(jnp.arange(entries.shape[position]) // (entries.shape[position] // shards_of)).reshape([-1 if axis == position else 1 for axis in range(entries.ndim)]) for position in (source, target)]
    chosen = jax.random.permutation(key, shards_of)[partner]
    strong = (owner == chosen) | (owner == (partner + shards_of // 2) % shards_of)
    return jnp.where(strong, factor * entries, entries)


def block_levels(own_key, shape, split, smallest, top_value):
    level, own = 1.0, jax.random.fold_in(own_key, 6)
    for position, shards_of in split:
        draws = jnp.exp(jax.random.uniform(jax.random.fold_in(own, position), (shards_of,), jnp.float32, smallest / len(split), top_value / len(split)))
        level = level * jnp.repeat(draws, shape[position] // shards_of).reshape([-1 if axis == position else 1 for axis in range(len(shape))])
    return level


def bell_draw(key, dims, spread, reach, pieces=(), kind=jnp.bfloat16):
    gain = block_levels(key, dims, pieces, -0.22, 0.18) if pieces else 1.0
    entries = jax.random.normal(key, dims, jnp.float32) * spread * gain
    return jnp.minimum(jnp.maximum(entries, -reach), reach).astype(kind)


def noise_with(stream_key, shape, deviation, bound, pieces, heavy, kind=jnp.bfloat16):
    array = deviation * jax.random.normal(stream_key, shape, jnp.float32)
    if pieces:
        array = array * block_levels(stream_key, shape, pieces, -0.22, 0.18)
    return jnp.clip(spiked(array, jax.random.fold_in(stream_key, 3), *heavy), -bound, bound).astype(kind)


def setup_inputs(seed: int = 0) -> dict:
    streams_of = jax.random.split(jax.random.key(seed), 10)
    query_out = noise_with(streams_of[0], (KQ, D), D ** -0.5, 0.125, ((1, 32),), (1, 0, 32, 2.75))
    query_in = bell_draw(streams_of[1], (KQ, FF), FF ** -0.5, 0.046875, ((1, 8),))
    eigen_out = bell_draw(streams_of[2], (D, D), D ** -0.5, 0.0625, ((0, 32), (1, 8)))
    eigen_in = bell_draw(streams_of[3], (FF, FF), FF ** -0.5, 0.046875, ((0, 8), (1, 32)))
    eigvals = draw_eigvals(jax.random.fold_in(streams_of[9], 71), 0)
    start = bell_draw(streams_of[5], (FF, NQ * RANK), 1.0, 6.0, ((0, 32),))
    grads_out = bell_draw(streams_of[6], (TOKENS, D), D ** -0.5, 0.0625, ((0, 32), (1, 8)))
    gate_pre = bell_draw(streams_of[7], (TOKENS, FF), 1.0, 6.0, ((0, 32), (1, 8)))
    up_pre = bell_draw(streams_of[8], (TOKENS, FF), FF ** -0.5, 0.046875, ((0, 32), (1, 8)))
    return {"query_out": query_out, "query_in": query_in, "eigen_out": eigen_out, "eigen_in": eigen_in, "eigvals": eigvals, "start": start, "grads_out": grads_out, "gate_pre": gate_pre, "up_pre": up_pre}


damping = 0.01
ridge_scale = 1e-06

def reference(query_out, query_in, eigen_out, eigen_in, eigvals, start, grads_out, gate_pre, up_pre):
    rot_out = jnp.dot(query_out.astype(jnp.float32), eigen_out.astype(jnp.float32), preferred_element_type=jnp.float32).astype(jnp.bfloat16)
    rot_in = jnp.dot(query_in.astype(jnp.float32), eigen_in.astype(jnp.float32), preferred_element_type=jnp.float32).astype(jnp.bfloat16)
    rot_out = rot_out.reshape(NQ, QTOK, D)
    rot_in = rot_in.reshape(NQ, QTOK, FF)
    start_cols = start.reshape(FF, NQ, RANK).transpose(1, 0, 2)
    identity = jnp.eye(RANK, dtype=jnp.float32)

    def precondition(operands):
        out_rows, in_rows, basis_in = operands
        rotated = jnp.dot(out_rows.T.astype(jnp.float32), in_rows.astype(jnp.float32), preferred_element_type=jnp.float32)
        rotated = (rotated / (eigvals + damping)).astype(jnp.bfloat16)
        basis_out = None
        for iteration in range(ITERS):
            image_cols = jnp.dot(rotated.astype(jnp.float32), basis_in.astype(jnp.float32), preferred_element_type=jnp.float32)
            gram_mat = jnp.dot(image_cols.T, image_cols, precision=lax.Precision.HIGHEST) / D
            gram_mat = gram_mat + ridge_scale * (jnp.trace(gram_mat) / RANK) * identity
            lower_factor = jnp.linalg.cholesky(gram_mat)
            inverse = jax.scipy.linalg.solve_triangular(lower_factor, identity, lower=True)
            basis_out = jnp.dot(image_cols, inverse.T, precision=lax.Precision.HIGHEST).astype(jnp.bfloat16)
            basis_in = jnp.dot(rotated.T.astype(jnp.float32), basis_out.astype(jnp.float32), preferred_element_type=jnp.float32).astype(jnp.bfloat16)
        return (basis_out, basis_in)
    basis_out, basis_in = lax.map(precondition, (rot_out, rot_in, start_cols))
    out_cols = basis_out.transpose(1, 0, 2).reshape(D, NQ * RANK)
    in_cols = basis_in.transpose(1, 0, 2).reshape(FF, NQ * RANK)
    out_factor = jnp.dot(eigen_out.astype(jnp.float32), out_cols.astype(jnp.float32), preferred_element_type=jnp.float32).astype(jnp.bfloat16)
    in_factor = jnp.dot(eigen_in.astype(jnp.float32), in_cols.astype(jnp.float32), preferred_element_type=jnp.float32).astype(jnp.bfloat16)
    hidden = (jax.nn.silu(gate_pre.astype(jnp.float32)) * up_pre.astype(jnp.float32)).astype(jnp.bfloat16)
    proj_out = jnp.dot(grads_out.astype(jnp.float32), out_factor.astype(jnp.float32), preferred_element_type=jnp.float32)
    proj_in = jnp.dot(hidden.astype(jnp.float32), in_factor.astype(jnp.float32), preferred_element_type=jnp.float32)
    scores = (proj_out * proj_in).reshape(TOKENS, NQ, RANK).sum(axis=2).T
    return (scores, out_factor, in_factor)
```

```python
import jax
import jax.numpy as jnp
from jax import lax
from jax.experimental import pallas as pl
from jax.experimental.pallas import tpu as pltpu
from jax.sharding import Mesh
from jax.sharding import PartitionSpec as P

D = 8192
NQ = 16
QTOK = 32
RANK = 16
ITERS = 2
NY = 4
NZ = 8
NW = 8
QR = NQ * RANK
KQ = NQ * QTOK
damping = 0.01
ridge_scale = 1e-06

GRP_DP = ("grp", "dp_0", "dp_1")
GRP_DP_WIDTH = ("grp", "dp_0", "dp_1", "width")
MESH = pl.DeviceIdType.MESH
BF = jnp.bfloat16
F32 = jnp.float32
HIGHEST = lax.Precision.HIGHEST

Y_ORDER = (2, 1, 3)
Z_ORDER = (4, 3, 5, 2, 6, 1, 7)
W_ORDER = (4, 5, 3, 2, 6, 7, 1)
N_SEMS = 320

NN = (((1,), (0,)), ((), ()))
NT = (((1,), (1,)), ((), ()))
TN = (((0,), (0,)), ((), ()))


def mm(a, b, dims, precision=None):
    return lax.dot_general(a, b, dims, precision=precision, preferred_element_type=F32)


def rows_at(start, size):
    return pl.ds(pl.multiple_of(start, size), size)


def inverse_of_factor(gram):
    row = lax.broadcasted_iota(jnp.int32, (RANK, RANK), 0)
    col = lax.broadcasted_iota(jnp.int32, (RANK, RANK), 1)
    eye = (row == col).astype(F32)
    trace_mean = jnp.sum(gram * eye, keepdims=True) / RANK
    left = gram + ridge_scale * trace_mean * eye
    right = eye
    for k in range(RANK):
        scale = 1.0 / jnp.sqrt(left[k : k + 1, k : k + 1])
        row_left = left[k : k + 1, :] * scale
        row_right = right[k : k + 1, :] * scale
        column = jnp.where(row[:, :1] > k, left[:, k : k + 1] * scale, 0.0)
        left = left - column * row_left
        right = jnp.where(row == k, row_right, right - column * row_right)
    return right


def layout_of(shapes):
    rows = shapes["eo"][0]
    width_rows = shapes["eo"][1]
    ff_w, ff_r = shapes["ei"]
    tokens = shapes["go"][0]
    fp = -(-ff_r // 128) * 128
    scratch = dict(
        qo=(shapes["qo"], BF),
        qi=(shapes["qi"], BF),
        eo=(shapes["eo"], BF),
        ei=(shapes["ei"], BF),
        ev=(shapes["ev"], F32),
        st=(shapes["st"], BF),
        go=(shapes["go"], BF),
        ga=(shapes["ga"], BF),
        up=(shapes["up"], BF),
        hid=(shapes["ga"], BF),
        inv=((width_rows, fp), F32),
        rot=((NQ, width_rows, fp), BF),
        ro_send=((KQ, width_rows), BF),
        ro_recv=((NY - 1, KQ // NY, width_rows), BF),
        ro_z=((KQ // NY, width_rows), BF),
        ro_zrecv=((NZ - 1, KQ // 32, width_rows), BF),
        ro=((KQ, width_rows), BF),
        ri_send=((KQ, fp), BF),
        ri_recv=((NW - 1, KQ // NW, fp), BF),
        ri=((KQ, fp), BF),
        bi0=((QR, fp), BF),
    )
    for it in range(ITERS):
        scratch |= {
            f"im_send{it}": ((QR, width_rows), BF),
            f"im_recv{it}": ((NY - 1, QR // NY, width_rows), BF),
            f"im_z{it}": ((QR // NY, width_rows), BF),
            f"im_zrecv{it}": ((NZ - 1, RANK, width_rows // 2), BF),
            f"gram{it}": ((2 * NW, RANK, RANK), F32),
            f"bo{it}": ((QR, width_rows), BF),
            f"re_send{it}": ((QR, fp), BF),
            f"re_recv{it}": ((NW - 1, QR // NW, fp), BF),
            f"bi{it + 1}": ((QR, fp), BF),
        }
    scratch |= dict(
        of_send=((rows, QR), BF),
        of_recv=((NW - 1, rows // NW, QR), BF),
        of_part=((rows // NW, QR), BF),
        of_block=((rows, QR), BF),
        of=((width_rows, QR), BF),
        if_send=((ff_w, QR), BF),
        if_recv=((NY - 1, ff_w // NY, QR), BF),
        if_z=((ff_w // NY, QR), BF),
        if_zrecv=((NZ - 1, ff_w // 16, QR // 2), BF),
        inf=((ff_w, QR), BF),
        po_send=((tokens, QR), BF),
        po_recv=((NW - 1, tokens // NW, QR), BF),
        pi_send=((tokens, QR), BF),
        pi_recv=((NW - 1, tokens // NW, QR), BF),
        sc=((NQ, tokens // NW), F32),
    )
    return scratch


INPUTS = ("qo", "qi", "eo", "ei", "ev", "st", "go", "ga", "up")
OUTPUTS = ("sc", "of", "inf")


def make_kernel(names):
    def kernel(*refs):
        hbm = dict(zip(INPUTS, refs))
        out = dict(zip(OUTPUTS, refs[len(INPUTS) :]))
        r = dict(zip(names, refs[len(INPUTS) + len(OUTPUTS) :]))
        send_sem, recv_sem, in_sem, out_sem = refs[-4:]

        zlo, y, zhi, w = (lax.axis_index(name) for name in GRP_DP_WIDTH)
        z = zhi * 4 + zlo
        width_rows = r["eo"].shape[1]
        ff_w, ff_r = r["ei"].shape
        fp = r["inv"].shape[1]
        tokens = r["go"].shape[0]

        def y_at(dy):
            return lax.rem(y + dy, NY)

        def z_at(dz):
            return lax.rem(z + dz, NZ)

        def w_at(dw):
            return lax.rem(w + dw, NW)

        def y_dev(dy):
            return (zlo, y_at(dy), zhi, w)

        def z_dev(dz):
            zz = z_at(dz)
            return (lax.rem(zz, 4), y, zz // 4, w)

        def w_dev(dw):
            return (zlo, y, zhi, w_at(dw))

        def pair_dev(dw):
            return (zlo + 1 - 2 * lax.rem(zlo, 2), y, zhi, w_at(dw))

        loads = {}
        for i, name in enumerate(("qo", "eo", "qi", "ei", "ev", "st", "ga", "up", "go")):
            loads[name] = pltpu.make_async_copy(hbm[name], r[name], in_sem.at[i])
            loads[name].start()

        barrier = pltpu.get_barrier_semaphore()
        partners = [y_dev(d) for d in Y_ORDER] + [z_dev(d) for d in Z_ORDER]
        partners += [w_dev(d) for d in W_ORDER] + [pair_dev(d) for d in range(1, NW)]
        for partner in partners:
            pl.semaphore_signal(barrier, inc=1, device_id=partner, device_id_type=MESH)

        count = [0]
        unsent = []

        def copy_to(src, dst, device):
            k = count[0]
            count[0] += 1
            return pltpu.make_async_remote_copy(
                src_ref=src,
                dst_ref=dst,
                send_sem=send_sem.at[k],
                recv_sem=recv_sem.at[k],
                device_id=device,
                device_id_type=MESH,
            )

        def send(src, dst, device):
            copy = copy_to(src, dst, device)
            copy.start()
            unsent.append(copy)
            return copy

        def arrive(copies):
            for copy in copies:
                copy.wait_recv()

        def sum_into(dst, own, own_at, recv, n, step):
            total = dst.shape[0]

            def body(i, carry):
                at = rows_at(i * step, step)
                acc = own[rows_at(own_at + i * step, step), :].astype(F32)
                for s in range(n):
                    acc = acc + recv[s, at, :].astype(F32)
                dst[at, :] = acc.astype(dst.dtype)
                return carry

            lax.fori_loop(0, total // step, body, 0)

        loads["qo"].wait()
        loads["eo"].wait()
        yrows = KQ // NY
        ro_y = []
        for dy in Y_ORDER + (0,):
            at = rows_at(y_at(dy) * yrows, yrows)
            part = mm(r["qo"][at, :], r["eo"][...], NN)
            r["ro_send"][at, :] = part.astype(BF)
            if dy == Y_ORDER[0]:
                pl.semaphore_wait(barrier, len(partners))
            if dy:
                ro_y.append(send(r["ro_send"].at[at, :], r["ro_recv"].at[dy - 1], y_dev(dy)))

        loads["qi"].wait()
        loads["ei"].wait()
        wrows = KQ // NW
        r["ri_send"][...] = jnp.zeros((KQ, fp), BF)

        def part_in(i, carry):
            at = rows_at(i * 128, 128)
            r["ri_send"][at, :ff_r] = mm(r["qi"][at, :], r["ei"][...], NN).astype(BF)
            return carry

        lax.fori_loop(0, KQ // 128, part_in, 0)
        ri_w = []
        for dw in W_ORDER:
            at = rows_at(w_at(dw) * wrows, wrows)
            ri_w.append(send(r["ri_send"].at[at, :], r["ri_recv"].at[dw - 1], w_dev(dw)))

        loads["ev"].wait()
        r["inv"][...] = jnp.zeros((width_rows, fp), F32)

        def invert(i, carry):
            at = rows_at(i * 64, 64)
            r["inv"][at, :ff_r] = 1.0 / (r["ev"][at, :] + damping)
            return carry

        lax.fori_loop(0, width_rows // 64, invert, 0)

        arrive(ro_y)
        sum_into(r["ro_z"], r["ro_send"], y * yrows, r["ro_recv"], NY - 1, 16)
        zrows = yrows // NZ
        ro_z = []
        for dz in Z_ORDER:
            at = rows_at(z_at(dz) * zrows, zrows)
            ro_z.append(send(r["ro_z"].at[at, :], r["ro_zrecv"].at[dz - 1], z_dev(dz)))

        arrive(ri_w)
        own_in = rows_at(w * wrows, wrows)
        sum_into(r["ri"].at[own_in, :], r["ri_send"], w * wrows, r["ri_recv"], NW - 1, 16)
        ri_g = [send(r["ri"].at[own_in, :], r["ri"].at[own_in, :], w_dev(dw)) for dw in W_ORDER]

        loads["st"].wait()
        r["bi0"][...] = jnp.zeros((QR, fp), BF)
        r["bi0"][:, :ff_r] = r["st"][...].astype(F32).T.astype(BF)

        arrive(ro_z)
        own_out = rows_at(y * yrows + z * zrows, zrows)
        sum_into(r["ro"].at[own_out, :], r["ro_z"], z * zrows, r["ro_zrecv"], NZ - 1, 16)
        ro_g = [send(r["ro"].at[own_out, :], r["ro"].at[own_out, :], z_dev(dz)) for dz in Z_ORDER]

        loads["ga"].wait()
        loads["up"].wait()

        def hide(i, carry):
            at = rows_at(i * 16, 16)
            gate = r["ga"][at, :].astype(F32)
            r["hid"][at, :] = (gate / (1.0 + jnp.exp(-gate)) * r["up"][at, :].astype(F32)).astype(BF)
            return carry

        lax.fori_loop(0, tokens // 16, hide, 0)

        arrive(ro_g)
        yblock = rows_at(y * yrows, yrows)
        ro_h = [send(r["ro"].at[yblock, :], r["ro"].at[yblock, :], y_dev(dy)) for dy in Y_ORDER]
        arrive(ri_g)
        arrive(ro_h)

        def rotate(q, carry):
            at = rows_at(q * QTOK, QTOK)
            part = mm(r["ro"][at, :], r["ri"][at, :], TN)
            r["rot"][q] = (part * r["inv"][...]).astype(BF)
            return carry

        lax.fori_loop(0, NQ, rotate, 0)

        per_y = NQ // NY
        per_w = NQ // NW
        half = width_rows // 2
        for it in range(ITERS):
            basis_in, im_send = r[f"bi{it}"], r[f"im_send{it}"]
            im_y = []
            for dy in Y_ORDER + (0,):
                yy = y_at(dy)

                def image(i, carry):
                    q = yy * per_y + i
                    at = rows_at(q * RANK, RANK)
                    im_send[at, :] = mm(basis_in[at, :], r["rot"][q], NT).astype(BF)
                    return carry

                lax.fori_loop(0, per_y, image, 0)
                if dy:
                    at = rows_at(yy * per_y * RANK, per_y * RANK)
                    im_y.append(
                        send(im_send.at[at, :], r[f"im_recv{it}"].at[dy - 1], y_dev(dy))
                    )
            arrive(im_y)
            im_z = r[f"im_z{it}"]
            sum_into(im_z, im_send, y * per_y * RANK, r[f"im_recv{it}"], NY - 1, 16)

            def piece(zz):
                return (
                    rows_at(zz // 2 * RANK, RANK),
                    pl.ds(pl.multiple_of(lax.rem(zz, 2) * half, half), half),
                )

            im_zs = []
            for dz in Z_ORDER:
                rows, cols = piece(z_at(dz))
                im_zs.append(
                    send(im_z.at[rows, cols], r[f"im_zrecv{it}"].at[dz - 1], z_dev(dz))
                )
            rows, cols = piece(z)
            arrive(im_zs)
            image_cols = im_z[rows, cols].astype(F32)
            for s in range(NZ - 1):
                image_cols = image_cols + r[f"im_zrecv{it}"][s].astype(F32)
            gram = r[f"gram{it}"]
            gram[0] = mm(image_cols, image_cols, NT, HIGHEST) / D
            grams = []
            for dw in W_ORDER + (0,):
                grams.append(send(gram.at[0], gram.at[2 * dw + 1], pair_dev(dw)))
                if dw:
                    grams.append(send(gram.at[0], gram.at[2 * dw], w_dev(dw)))
            arrive(grams)
            whole = gram[0]
            for s in range(1, 2 * NW):
                whole = whole + gram[s]
            inverse = inverse_of_factor(whole)
            bo = r[f"bo{it}"]
            bo_rows = rows_at(y * per_y * RANK + z // 2 * RANK, RANK)
            bo[bo_rows, cols] = mm(inverse, image_cols, NN, HIGHEST).astype(BF)
            bo_z = [send(bo.at[bo_rows, cols], bo.at[bo_rows, cols], z_dev(dz)) for dz in Z_ORDER]
            arrive(bo_z)
            mine = rows_at(y * per_y * RANK, per_y * RANK)
            bo_y = [send(bo.at[mine, :], bo.at[mine, :], y_dev(dy)) for dy in Y_ORDER]
            arrive(bo_y)

            re_send, next_in = r[f"re_send{it}"], r[f"bi{it + 1}"]
            re_w = []
            for dw in W_ORDER + (0,):
                ww = w_at(dw)

                def transposed(i, carry):
                    q = ww * per_w + i
                    at = rows_at(q * RANK, RANK)
                    re_send[at, :] = mm(bo[at, :], r["rot"][q], NN).astype(BF)
                    return carry

                lax.fori_loop(0, per_w, transposed, 0)
                if dw:
                    at = rows_at(ww * per_w * RANK, per_w * RANK)
                    re_w.append(
                        send(re_send.at[at, :], r[f"re_recv{it}"].at[dw - 1], w_dev(dw))
                    )
            if it == ITERS - 1:
                orows = r["eo"].shape[0] // NW
                r["of_send"][...] = mm(r["eo"][...], bo[...], NT).astype(BF)
                of_w = []
                for dw in W_ORDER:
                    at = rows_at(w_at(dw) * orows, orows)
                    of_w.append(send(r["of_send"].at[at, :], r["of_recv"].at[dw - 1], w_dev(dw)))
            arrive(re_w)
            own = rows_at(w * per_w * RANK, per_w * RANK)
            sum_into(next_in.at[own, :], re_send, w * per_w * RANK, r[f"re_recv{it}"], NW - 1, 16)
            re_g = [send(next_in.at[own, :], next_in.at[own, :], w_dev(dw)) for dw in W_ORDER]
            if it == ITERS - 1:
                arrive(of_w)
                sum_into(r["of_part"], r["of_send"], w * orows, r["of_recv"], NW - 1, 16)
                owner = 2 * zlo + y // 2
                at_w = rows_at(w * orows, orows)
                of_k = count[0]
                count[0] += NW
                away = lax.rem(owner - w + NW, NW)

                def to_owner(k):
                    return pltpu.make_async_remote_copy(
                        src_ref=r["of_part"],
                        dst_ref=r["of_block"].at[at_w, :],
                        send_sem=send_sem.at[of_k],
                        recv_sem=recv_sem.at[of_k + k],
                        device_id=(zlo, y, zhi, owner),
                        device_id_type=MESH,
                    )

                @pl.when(away != 0)
                def _():
                    to_owner(away).start()

                @pl.when(away == 0)
                def _():
                    r["of_block"][at_w, :] = r["of_part"][...]

            arrive(re_g)

        basis_in = r[f"bi{ITERS}"]
        frows = ff_w // NY
        fstep = frows // 4
        if_y = []
        for dy in Y_ORDER + (0,):
            yy = y_at(dy)

            def part_if(i, carry):
                at = pl.ds(pl.multiple_of(yy * frows + i * fstep, 16), fstep)
                r["if_send"][at, :] = mm(r["ei"][at, :], basis_in[:, :ff_r], NT).astype(BF)
                return carry

            lax.fori_loop(0, 4, part_if, 0)
            if dy:
                at = rows_at(yy * frows, frows)
                if_y.append(send(r["if_send"].at[at, :], r["if_recv"].at[dy - 1], y_dev(dy)))

        orows = r["eo"].shape[0]

        @pl.when(away == 0)
        def _():
            for k in range(1, NW):
                to_owner(k).wait_recv()

        @pl.when(away != 0)
        def _():
            to_owner(away).wait_send()

        of = r["of"]
        core = lax.rem(w, 2)
        x = w // 2
        column = core == y // 2
        blk = rows_at((lax.rem(y, 2) * 2 + zhi) * orows, orows)
        of_z0 = count[0]
        count[0] += 2 * (NZ - 1)

        def along_z(dz, zh):
            return pltpu.make_async_remote_copy(
                src_ref=of.at[blk, :],
                dst_ref=of.at[blk, :],
                send_sem=send_sem.at[of_z0 + dz - 1],
                recv_sem=recv_sem.at[of_z0 + zh],
                device_id=z_dev(dz),
                device_id_type=MESH,
            )

        @pl.when(away == 0)
        def _():
            of[blk, :] = r["of_block"][...]
            for dz in Z_ORDER:
                along_z(dz, zhi).start()

        for zh in range(2):

            @pl.when(jnp.logical_and(column, z != zh * 4 + x))
            def _(zh=zh):
                along_z(1, zh).wait_recv()

        of_y0 = count[0]
        count[0] += NY
        two = rows_at(lax.rem(y, 2) * 2 * orows, 2 * orows)

        def along_y(dy, k):
            return pltpu.make_async_remote_copy(
                src_ref=of.at[two, :],
                dst_ref=of.at[two, :],
                send_sem=send_sem.at[of_y0 + dy - 1],
                recv_sem=recv_sem.at[of_y0 + k],
                device_id=y_dev(dy),
                device_id_type=MESH,
            )

        @pl.when(column)
        def _():
            for dy in Y_ORDER:
                along_y(dy, lax.rem(y, 2)).start()

        arrive(if_y)
        fsum = pl.ds(0, frows)
        sum_into(r["if_z"].at[fsum, :], r["if_send"], y * frows, r["if_recv"], NY - 1, 64)

        def share(zz, base):
            return (
                pl.ds(pl.multiple_of(base + zz // 2 * fstep, 16), fstep),
                pl.ds(pl.multiple_of(lax.rem(zz, 2) * (QR // 2), QR // 2), QR // 2),
            )

        if_zs = []
        for dz in Z_ORDER:
            rows, cols = share(z_at(dz), 0)
            if_zs.append(send(r["if_z"].at[rows, cols], r["if_zrecv"].at[dz - 1], z_dev(dz)))
        arrive(if_zs)
        rows, cols = share(z, 0)
        acc = r["if_z"][rows, cols].astype(F32)
        for s in range(NZ - 1):
            acc = acc + r["if_zrecv"][s].astype(F32)
        inf = r["inf"]
        rows, cols = share(z, y * frows)
        inf[rows, cols] = acc.astype(BF)
        if_g = [send(inf.at[rows, cols], inf.at[rows, cols], z_dev(dz)) for dz in Z_ORDER]

        for k in range(2):

            @pl.when(y != 2 * core + k)
            def _(k=k):
                along_y(1, k).wait_recv()

        loads["go"].wait()
        out_copy = pltpu.make_async_copy(of, out["of"], out_sem.at[0])
        out_copy.start()
        trows = tokens // NW

        def project_out(i, carry):
            at = rows_at(i * 128, 128)
            r["po_send"][at, :] = mm(r["go"][at, :], of[...], NN).astype(BF)
            return carry

        lax.fori_loop(0, tokens // 128, project_out, 0)
        po_w = []
        for dw in W_ORDER:
            at = rows_at(w_at(dw) * trows, trows)
            po_w.append(send(r["po_send"].at[at, :], r["po_recv"].at[dw - 1], w_dev(dw)))

        arrive(if_g)
        block = rows_at(y * frows, frows)
        if_h = [send(inf.at[block, :], inf.at[block, :], y_dev(dy)) for dy in Y_ORDER]
        arrive(if_h)
        in_copy = pltpu.make_async_copy(inf, out["inf"], out_sem.at[1])
        in_copy.start()

        def project_in(i, carry):
            at = rows_at(i * 128, 128)
            r["pi_send"][at, :] = mm(r["hid"][at, :], inf[...], NN).astype(BF)
            return carry

        lax.fori_loop(0, tokens // 128, project_in, 0)
        pi_w = []
        for dw in W_ORDER:
            at = rows_at(w_at(dw) * trows, trows)
            pi_w.append(send(r["pi_send"].at[at, :], r["pi_recv"].at[dw - 1], w_dev(dw)))
        arrive(po_w)
        arrive(pi_w)
        own = rows_at(w * trows, trows)
        proj_out = r["po_send"][own, :].astype(F32)
        proj_in = r["pi_send"][own, :].astype(F32)
        for s in range(NW - 1):
            proj_out = proj_out + r["po_recv"][s].astype(F32)
            proj_in = proj_in + r["pi_recv"][s].astype(F32)
        of_query = lax.broadcasted_iota(jnp.int32, (NQ, QR), 1) // RANK
        chosen = (of_query == lax.broadcasted_iota(jnp.int32, (NQ, QR), 0)).astype(F32)
        r["sc"][...] = mm(chosen, proj_out * proj_in, NT, HIGHEST)
        score_copy = pltpu.make_async_copy(r["sc"], out["sc"], out_sem.at[2])
        score_copy.start()

        for copy in unsent:
            copy.wait_send()

        @pl.when(away == 0)
        def _():
            for dz in Z_ORDER:
                along_z(dz, zhi).wait_send()

        @pl.when(column)
        def _():
            for dy in Y_ORDER:
                along_y(dy, lax.rem(y, 2)).wait_send()

        out_copy.wait()
        in_copy.wait()
        score_copy.wait()
        assert count[0] <= N_SEMS, count[0]

    return kernel


def per_device(
    query_out, query_in, eigen_out, eigen_in, eigvals, start, grads_out, gate_pre, up_pre
):
    args = (query_out, query_in, eigen_out, eigen_in, eigvals, start, grads_out, gate_pre, up_pre)
    shapes = {name: a.shape for name, a in zip(INPUTS, args)}
    scratch = layout_of(shapes)
    tokens = grads_out.shape[0]
    return pl.pallas_call(
        make_kernel(tuple(scratch)),
        out_shape=(
            jax.ShapeDtypeStruct((NQ, tokens // NW), F32),
            jax.ShapeDtypeStruct((eigen_out.shape[1], QR), BF),
            jax.ShapeDtypeStruct((eigen_in.shape[0], QR), BF),
        ),
        in_specs=[pl.BlockSpec(memory_space=pl.ANY)] * len(INPUTS),
        out_specs=(pl.BlockSpec(memory_space=pl.ANY),) * len(OUTPUTS),
        scratch_shapes=[pltpu.VMEM(shape, dtype) for shape, dtype in scratch.values()]
        + [
            pltpu.SemaphoreType.DMA((N_SEMS,)),
            pltpu.SemaphoreType.DMA((N_SEMS,)),
            pltpu.SemaphoreType.DMA((len(INPUTS),)),
            pltpu.SemaphoreType.DMA((len(OUTPUTS),)),
        ],
        compiler_params=pltpu.CompilerParams(
            collective_id=0, has_side_effects=True, vmem_limit_bytes=60 * 1024 * 1024
        ),
    )(*args)


def solution(mesh):
    finer = Mesh(
        mesh.devices.reshape(mesh.shape["grp"], 4, 2, mesh.shape["width"]), GRP_DP_WIDTH
    )
    placed = (
        P(None, GRP_DP),
        P(None, "width"),
        P(GRP_DP, "width"),
        P("width", GRP_DP),
        P("width", GRP_DP),
        P(GRP_DP, None),
        P(GRP_DP, "width"),
        P(GRP_DP, "width"),
        P(GRP_DP, "width"),
    )
    return jax.shard_map(
        per_device,
        mesh=finer,
        in_specs=placed,
        out_specs=(P(None, GRP_DP_WIDTH), P("width", None), P("width", None)),
        check_vma=False,
    )
```
